128 devices in a mesh: fsdp: 32 (over x, z, core), panel: 4 (over y).
Axes of the slice: x: 4, y: 4, z: 4, core: 2. Of those that a mesh axis runs over, the one named last changes fastest.
Arguments:
- gradients: bfloat16 [3, 4096, 11008], P(None, ('fsdp', 'panel')), may hold values from -80 to 80
- test_matrix: bfloat16 [11008, 512], replicated, may hold values from -0.0546875 to 0.0546875
- first_moment: float32 [3, 512, 11008], P(None, 'panel', 'fsdp'), may hold values from -5 to 5
- second_moment: float32 [3, 512, 11008], P(None, 'panel', 'fsdp'), may hold values from 0.05 to 5
Outputs:
- subspace: float32 [3, 4096, 512], P(None, ('fsdp', 'panel'))
- new_first: float32 [3, 512, 11008], P(None, 'panel', 'fsdp')
- new_second: float32 [3, 512, 11008], P(None, 'panel', 'fsdp')
- weight_delta: bfloat16 [3, 4096, 11008], P(None, ('fsdp', 'panel'))
The draws below stay inside these ranges and needn't reach their ends.
All inputs are finite; a program needn't handle non-finite values.
Results may differ from the reference program's by a relative error of at most 0.017.
Values may be sent and summed in bfloat16 or wider, within the bound.
No kernel may reach another device: no remote copies, remote signals or barrier semaphores. Data moves between devices by JAX's collectives and lax.ppermute only.
A program may use at most 128 MiB of HBM per device.

```python
import math
import jax
import jax.numpy as jnp
from jax import lax

D = 4096
FF = 11008
RANK = 512
LAYERS = 3


def draw_gradients(key, part):
    key_noise = jax.random.fold_in(key, 11)
    key_rows = jax.random.fold_in(key, 12)
    key_cols = jax.random.fold_in(key, 13)
    row_logs = jax.random.uniform(key_rows, (LAYERS, D, 1), minval=0.0, maxval=1.0)
    row_place = jnp.arange(D, dtype=jnp.float32)[None, :, None] / D
    row_scale = jnp.power(10.0, row_logs) * jnp.sqrt(1.0 + 2.0 * row_place)
    col_scale = jnp.power(10.0, jax.random.uniform(key_cols, (LAYERS, 1, FF), minval=0.0, maxval=1.0))
    noise = jnp.clip(jax.random.normal(key_noise, (LAYERS, D, FF), dtype=jnp.float32), -4.0, 4.0)
    return (noise * row_scale * col_scale / 10.0).astype(jnp.bfloat16)


def block_scale(rng, dims, cuts, smallest, high):
    gain = 1.0
    for dim, blocks in cuts:
        draws = jax.random.uniform(jax.random.fold_in(jax.random.fold_in(rng, 6), dim), (blocks,), jnp.float32, smallest / len(cuts), high / len(cuts))
        gain = gain * jnp.repeat(jnp.exp(draws), dims[dim] // blocks).reshape((-1,) + (1,) * (len(dims) - 1 - dim))
    return gain


def scatter_about(own_key, dims, scale, limit, split=(), kind=jnp.bfloat16):
    drawn = jax.random.normal(own_key, dims, jnp.float32) * scale
    if len(split) > 0:
        drawn = block_scale(own_key, dims, split, -0.22, 0.18) * drawn
    return jnp.clip(drawn, min=-limit, max=limit).astype(kind)


def setup_inputs(seed: int = 0) -> dict:
    key_of = jax.random.split(jax.random.key(seed), 5)
    gradients = draw_gradients(jax.random.fold_in(key_of[4], 71), 0)
    test_matrix = scatter_about(key_of[1], (FF, RANK), FF ** -0.5, 0.0546875)
    first_moment = scatter_about(key_of[2], (LAYERS, RANK, FF), 1.0, 5.0, ((1, 4), (2, 32)), jnp.float32)
    second_moment = jnp.clip(jnp.exp(math.log(5.0) - 4.6051702 * jax.random.uniform(key_of[3], (LAYERS, RANK, FF), jnp.float32) ** block_scale(key_of[3], (LAYERS, RANK, FF), ((1, 4), (2, 32)), -0.2, 0.2)), 0.05, 5.0)
    return {"gradients": gradients, "test_matrix": test_matrix, "first_moment": first_moment, "second_moment": second_moment}


def one_layer(gradient, test_matrix, first_moment, second_moment):
    sketch = jnp.dot(gradient.astype(jnp.float32), test_matrix.astype(jnp.float32), preferred_element_type=jnp.float32)
    gram_matrix = jnp.dot(sketch.T, sketch, precision=lax.Precision.HIGHEST) / D
    factor = jnp.linalg.cholesky(gram_matrix)
    subspace = jax.scipy.linalg.solve_triangular(factor, sketch.T, lower=True).T
    basis_half = subspace.astype(jnp.bfloat16)
    projected = jnp.dot(basis_half.T.astype(jnp.float32), gradient.astype(jnp.float32), preferred_element_type=jnp.float32) / math.sqrt(D)
    new_first = 0.9 * first_moment + 0.1 * projected
    new_second = 0.95 * second_moment + 0.05 * projected * projected
    update = (new_first / (jnp.sqrt(new_second) + 1e-08)).astype(jnp.bfloat16)
    weight_delta = (jnp.dot(basis_half.astype(jnp.float32), update.astype(jnp.float32), preferred_element_type=jnp.float32) / math.sqrt(D)).astype(jnp.bfloat16)
    return (subspace, new_first, new_second, weight_delta)

def reference(gradients, test_matrix, first_moment, second_moment):
    results = [one_layer(gradients[layer], test_matrix, first_moment[layer], second_moment[layer]) for layer in range(LAYERS)]
    subspace = jnp.stack([item[0] for item in results])
    new_first = jnp.stack([item[1] for item in results])
    new_second = jnp.stack([item[2] for item in results])
    weight_delta = jnp.stack([item[3] for item in results])
    return (subspace, new_first, new_second, weight_delta)
```

```python
import jax
import jax.numpy as jnp
from jax import lax
from jax.experimental import pallas as pl
from jax.experimental.pallas import tpu as pltpu
from jax.sharding import PartitionSpec as P

D = 4096
ROOT = 64.0
NX, NZ, NC, NP = 4, 4, 2, 4
BLK, VR = 128, 8
HI = lax.Precision.HIGHEST
F32, BF16 = jnp.float32, jnp.bfloat16


def fsdp_id(x, z, c):
    return (x * NZ + z) * NC + c


def shift_x(v, s):
    pairs = [(fsdp_id(x, z, c), fsdp_id((x + s) % NX, z, c)) for x in range(NX) for z in range(NZ) for c in range(NC)]
    return lax.ppermute(v, "fsdp", pairs)


def shift_z(v, s):
    pairs = [(fsdp_id(x, z, c), fsdp_id(x, (z + s) % NZ, c)) for x in range(NX) for z in range(NZ) for c in range(NC)]
    return lax.ppermute(v, "fsdp", pairs)


def swap_core(v):
    return lax.ppermute(v, "fsdp", [(f, f ^ 1) for f in range(NX * NZ * NC)])


def shift_y(v, s, keep=lambda src, dst: True):
    pairs = [(p, (p + s) % NP) for p in range(NP)]
    return lax.ppermute(v, "panel", [pr for pr in pairs if keep(*pr)])


def gather_shift(v, shift, n):
    return jnp.stack([v] + [shift(v, s) for s in range(1, n)])


def dotf(a, b, ca, cb):
    return lax.dot_general(a, b, (((ca,), (cb,)), ((), ())), precision=HI, preferred_element_type=F32)


def rem(a, n):
    return lax.rem(a + n, n)


def gram_kernel(pos_ref, s0_ref, s1_ref, s2_ref, s3_ref, t_ref, o_ref, s_ref, g_ref):
    c, x, z = pos_ref[0], pos_ref[1], pos_ref[2]
    rows = s0_ref.shape[0]
    for k, ref in enumerate((s0_ref, s1_ref, s2_ref, s3_ref)):
        s_ref[k * rows : (k + 1) * rows, :] = ref[...]
    s_ref[4 * rows :, :] = t_ref[...]

    def blocks(i, j):
        cols = s_ref[...]
        wi = cols.shape[1] - i * BLK
        g_ref[:, :wi] = dotf(cols[:, i * BLK : (i + 1) * BLK], cols[:, i * BLK :], 0, 0)
        g_ref[:, wi:] = dotf(cols[:, j * BLK : (j + 1) * BLK], cols[:, j * BLK :], 0, 0)

    @pl.when(c == 0)
    def _():
        blocks(0, 3)

    @pl.when(c != 0)
    def _():
        blocks(1, 2)

    for xx in range(NX):
        for zz in range(NZ):
            r = (xx * NZ + zz) * VR
            o_ref[rem(xx - x, NX), rem(zz - z, NZ)] = g_ref[r : r + VR, :] * (1.0 / D)


def gram_share(pos, parts, other):
    rows = parts[0].shape[0]
    n = parts[0].shape[1]
    return pl.pallas_call(
        gram_kernel,
        out_shape=jax.ShapeDtypeStruct((NX, NZ, VR, 5 * BLK), F32),
        in_specs=[pl.BlockSpec(memory_space=pltpu.SMEM)] + [pl.BlockSpec(memory_space=pltpu.VMEM)] * 5,
        scratch_shapes=[pltpu.VMEM((8 * rows, n), F32), pltpu.VMEM((BLK, 5 * BLK), F32)],
        name="gram",
    )(pos, *parts, other)


def factor_block(tiles, out_ref):
    nt = len(tiles)
    lane = lax.broadcasted_iota(jnp.int32, (VR, BLK), 1)
    sub = lax.broadcasted_iota(jnp.int32, (VR, BLK), 0)
    tiles = list(tiles)
    for b in range(nt):
        c = VR * b
        t = tiles[b]
        inblk = (lane >= c) & (lane < c + VR)
        cols = [jnp.broadcast_to(t[:, c + j : c + j + 1], (VR, BLK)) for j in range(VR)]
        e = [[jnp.broadcast_to(cols[j][i : i + 1, :], (VR, BLK)) if i >= j else None for j in range(VR)] for i in range(VR)]
        start = jnp.where(inblk, (lane - c == sub).astype(F32), t)
        rows = [jnp.broadcast_to(start[j : j + 1, :], (VR, BLK)) for j in range(VR)]
        m = [[None] * VR for _ in range(VR)]
        r = [None] * VR
        for j in range(VR):
            r[j] = 1.0 / e[j][j]
            for i in range(j + 1, VR):
                m[i][j] = e[i][j] * r[j]
            for i in range(j + 1, VR):
                for k in range(i, VR):
                    e[k][i] = e[k][i] - m[k][j] * e[i][j]
            for i in range(j + 1, VR):
                rows[i] = rows[i] - m[i][j] * rows[j]
        for j in range(VR):
            out_ref[c + j : c + j + 1, :] = (rows[j] * lax.rsqrt(e[j][j]))[0:1, :]
        for s in range(b + 1, nt):
            q = [jnp.broadcast_to(tiles[s][:, c + j : c + j + 1], (VR, BLK)) for j in range(VR)]
            acc = jnp.where(inblk, 0.0, tiles[s])
            for j in range(VR):
                for i in range(j + 1, VR):
                    q[i] = q[i] - q[j] * m[i][j]
                acc = acc - (q[j] * r[j]) * rows[j]
            tiles[s] = acc


def chol_kernel(pos_ref, ga_ref, gb_ref, s0_ref, s1_ref, s2_ref, s3_ref, o_ref, a_ref, x_ref, w_ref):
    c, x, z = pos_ref[0], pos_ref[1], pos_ref[2]
    n = a_ref.shape[0]
    nb = n // BLK
    rows = s0_ref.shape[0]

    def place(src, i, j):
        wi = n - i * BLK
        for xx in range(NX):
            for zz in range(NZ):
                r = (xx * NZ + zz) * VR
                piece = src[rem(x - xx, NX), rem(z - zz, NZ)]
                a_ref[i * BLK + r : i * BLK + r + VR, i * BLK :] = piece[:, :wi]
                a_ref[j * BLK + r : j * BLK + r + VR, j * BLK :] = piece[:, wi:]

    @pl.when(c == 0)
    def _():
        place(ga_ref, 0, 3)
        place(gb_ref, 1, 2)

    @pl.when(c != 0)
    def _():
        place(gb_ref, 0, 3)
        place(ga_ref, 1, 2)

    for k, ref in enumerate((s0_ref, s1_ref, s2_ref, s3_ref)):
        x_ref[k * rows : (k + 1) * rows, :] = ref[...]
    low = lax.broadcasted_iota(jnp.int32, (BLK, BLK), 0) >= lax.broadcasted_iota(jnp.int32, (BLK, BLK), 1)
    for ob in range(nb):
        lo = ob * BLK
        hi = lo + BLK
        factor_block([a_ref[lo + VR * i : lo + VR * i + VR, lo:hi] for i in range(BLK // VR)], w_ref)
        w = jnp.where(low, w_ref[...], 0.0)
        xo = dotf(x_ref[:, lo:hi], w, 1, 1)
        if ob + 1 < nb:
            u = dotf(w, a_ref[lo:hi, hi:], 1, 0)
            for ib in range(ob + 1, nb):
                off = (ib - ob - 1) * BLK
                a_ref[ib * BLK : (ib + 1) * BLK, ib * BLK :] -= dotf(u[:, off : off + BLK], u[:, off:], 0, 0)
            x_ref[:, hi:] -= dotf(xo, u, 1, 0)
        for k in range(4):
            o_ref[k, :, lo:hi] = xo[k * rows : (k + 1) * rows, :]


def chol_basis(pos, ga, gb, parts):
    rows, n = parts[0].shape
    return pl.pallas_call(
        chol_kernel,
        out_shape=jax.ShapeDtypeStruct((4, rows, n), F32),
        in_specs=[pl.BlockSpec(memory_space=pltpu.SMEM)] + [pl.BlockSpec(memory_space=pltpu.VMEM)] * 6,
        scratch_shapes=[pltpu.VMEM((n, n), F32), pltpu.VMEM((4 * rows, n), F32), pltpu.VMEM((BLK, BLK), F32)],
        cost_estimate=pl.CostEstimate(flops=20_000_000_000, bytes_accessed=40_000_000, transcendentals=1024),
        name="cholesky_basis",
    )(pos, ga, gb, *parts)


def project_kernel(pos_ref, ba_ref, bb_ref, g_ref, b_ref, own_ref, send_ref, p_ref):
    c, x, z, p = pos_ref[0], pos_ref[1], pos_ref[2], pos_ref[3]
    rows = ba_ref.shape[2]

    def place(ref, cc):
        for xx in range(NX):
            for zz in range(NZ):
                r = fsdp_id(xx, zz, cc) * rows
                b_ref[r : r + rows, :] = ref[rem(x - xx, NX), rem(z - zz, NZ)]

    @pl.when(c == 0)
    def _():
        place(ba_ref, 0)
        place(bb_ref, 1)

    @pl.when(c != 0)
    def _():
        place(bb_ref, 0)
        place(ba_ref, 1)

    p_ref[...] = lax.dot_general(b_ref[...], g_ref[...], (((0,), (0,)), ((), ())), preferred_element_type=F32)
    share = own_ref.shape[0]
    own_ref[...] = p_ref[pl.ds(pl.multiple_of(p * share, share), share), :]
    for s in range(1, NP):
        row = pl.multiple_of(rem(p + s, NP) * share, share)
        send_ref[s - 1] = p_ref[pl.ds(row, share), :].astype(BF16)


def project(pos, ba, bb, g):
    rows, n = ba.shape[2], ba.shape[3]
    w = g.shape[1]
    share = n // NP
    return pl.pallas_call(
        project_kernel,
        out_shape=(
            jax.ShapeDtypeStruct((g.shape[0], n), BF16),
            jax.ShapeDtypeStruct((share, w), F32),
            jax.ShapeDtypeStruct((NP - 1, share, w), BF16),
        ),
        in_specs=[pl.BlockSpec(memory_space=pltpu.SMEM)] + [pl.BlockSpec(memory_space=pltpu.VMEM)] * 3,
        scratch_shapes=[pltpu.VMEM((n, w), F32)],
        name="project",
    )(pos, ba, bb, g)


def delta_kernel(pos_ref, b_ref, u0_ref, u1_ref, u2_ref, u3_ref, o_ref, u_ref):
    p = pos_ref[3]
    share = u0_ref.shape[0]
    for s, ref in enumerate((u0_ref, u1_ref, u2_ref, u3_ref)):
        u_ref[pl.ds(pl.multiple_of(rem(p - s, NP) * share, share), share), :] = ref[...]
    d = lax.dot_general(b_ref[...], u_ref[...], (((1,), (0,)), ((), ())), preferred_element_type=F32)
    o_ref[...] = (d * (1.0 / ROOT)).astype(BF16)


def delta_block(pos, basis_cols, ups):
    share, w = ups[0].shape
    return pl.pallas_call(
        delta_kernel,
        out_shape=jax.ShapeDtypeStruct((basis_cols.shape[0], w), BF16),
        in_specs=[pl.BlockSpec(memory_space=pltpu.SMEM)] + [pl.BlockSpec(memory_space=pltpu.VMEM)] * 5,
        scratch_shapes=[pltpu.VMEM((NP * share, w), BF16)],
        name="delta",
    )(pos, basis_cols, *ups)


def per_device(gradients, test_matrix, first_moment, second_moment):
    layers, local_rows, col_width = gradients.shape
    rank = test_matrix.shape[1]
    f = lax.axis_index("fsdp")
    p = lax.axis_index("panel")
    c, z, x = f % NC, (f // NC) % NZ, f // (NC * NZ)
    pos = jnp.stack([c, x, z, p]).astype(jnp.int32)

    sketches = jnp.dot(gradients.reshape(layers * local_rows, col_width), test_matrix, preferred_element_type=F32)
    sketches = sketches.reshape(layers, local_rows, rank)

    def layer_rows(l):
        return lax.dynamic_index_in_dim(sketches, jnp.minimum(l, layers - 1), 0, keepdims=False)

    parts = [layer_rows(p)]
    parts += [shift_y(layer_rows((p + s) % NP), s, lambda src, dst: dst < layers) for s in range(1, NP)]
    other = swap_core(jnp.concatenate(parts))
    share = gram_share(pos, parts, other)
    share = share[0] + sum(shift_x(share[s], s) for s in range(1, NX))
    share = share[0] + sum(shift_z(share[s], s) for s in range(1, NZ))
    share = gather_shift(share, shift_z, NZ)
    share = gather_shift(share, shift_x, NX)
    basis = chol_basis(pos, share, swap_core(share), parts)
    back = jnp.stack([basis[0]] + [shift_y(basis[s], NP - s, lambda src, dst: src < layers) for s in range(1, NP)])

    blocks = lax.all_to_all(gradients, "fsdp", split_axis=2, concat_axis=1, tiled=True)
    basis_list, firsts, seconds, deltas = [], [], [], []
    for layer in range(layers):
        local = lax.dynamic_index_in_dim(back, rem(layer - p, NP), 0, keepdims=False)
        half = local.astype(BF16)
        half = gather_shift(gather_shift(half, shift_z, NZ), shift_x, NX)
        basis_cols, own, send = project(pos, half, swap_core(half), blocks[layer])
        total = own + sum(shift_y(send[s - 1], s).astype(F32) for s in range(1, NP))
        projected = total * (1.0 / ROOT)
        first_out = 0.9 * first_moment[layer] + 0.1 * projected
        second_out = 0.95 * second_moment[layer] + 0.05 * projected * projected
        update = (first_out / (jnp.sqrt(second_out) + 1e-08)).astype(BF16)
        ups = [update] + [shift_y(update, s) for s in range(1, NP)]
        delta = delta_block(pos, basis_cols, ups)
        deltas.append(lax.all_to_all(delta, "fsdp", split_axis=0, concat_axis=1, tiled=True))
        basis_list.append(local)
        firsts.append(first_out)
        seconds.append(second_out)
    return (jnp.stack(basis_list), jnp.stack(firsts), jnp.stack(seconds), jnp.stack(deltas))


def solution(mesh):
    return jax.shard_map(
        per_device,
        mesh=mesh,
        in_specs=(
            P(None, ("fsdp", "panel"), None),
            P(),
            P(None, "panel", "fsdp"),
            P(None, "panel", "fsdp"),
        ),
        out_specs=(
            P(None, ("fsdp", "panel"), None),
            P(None, "panel", "fsdp"),
            P(None, "panel", "fsdp"),
            P(None, ("fsdp", "panel"), None),
        ),
        check_vma=False,
    )
```

```python
import jax
import jax.numpy as jnp
from jax import lax
from jax.experimental import pallas as pl
from jax.experimental.pallas import tpu as pltpu
from jax.sharding import PartitionSpec as P

D = 4096
ROOT = 64.0
NX, NZ, NC, NP = 4, 4, 2, 4
NF = NX * NZ * NC
BLK, VR = 128, 8
HI = lax.Precision.HIGHEST
F32, BF16 = jnp.float32, jnp.bfloat16
SMEM_SPEC = pl.BlockSpec(memory_space=pltpu.SMEM)
VMEM_SPEC = pl.BlockSpec(memory_space=pltpu.VMEM)
ANY_SPEC = pl.BlockSpec(memory_space=pl.ANY)


SAME_CORE = [[NC * i + c for i in range(NX * NZ)] for c in range(NC)]


def swap_core(v):
    return lax.ppermute(v, "fsdp", [(f, f ^ 1) for f in range(NF)])


def exchange(v, axes, groups=None):
    return lax.all_to_all(v, axes, split_axis=0, concat_axis=0, tiled=True, axis_index_groups=groups)


def dotf(a, b, ca, cb):
    return lax.dot_general(a, b, (((ca,), (cb,)), ((), ())), precision=HI, preferred_element_type=F32)


def dotb(a, b, ca, cb):
    return lax.dot_general(a, b, (((ca,), (cb,)), ((), ())), preferred_element_type=F32)


def cut_kernel(g_ref, o_ref):
    w = o_ref.shape[3]
    for f in range(o_ref.shape[0]):
        o_ref[f, 0] = g_ref[0, :, f * w : (f + 1) * w]


def cut_columns(g):
    layers, rows, width = g.shape
    w = width // NF
    return pl.pallas_call(
        cut_kernel,
        grid=(layers,),
        out_shape=jax.ShapeDtypeStruct((NF, NP, rows, w), BF16),
        in_specs=[pl.BlockSpec((1, rows, width), lambda l: (l, 0, 0))],
        out_specs=pl.BlockSpec((NF, 1, rows, w), lambda l: (0, l, 0, 0)),
        name="cut_columns",
    )(g)


def join_kernel(d_ref, o_ref):
    w = d_ref.shape[3]
    for f in range(d_ref.shape[0]):
        o_ref[0, :, f * w : (f + 1) * w] = d_ref[f, 0]


def join_columns(d, layers):
    nf, _, rows, w = d.shape
    return pl.pallas_call(
        join_kernel,
        grid=(layers,),
        out_shape=jax.ShapeDtypeStruct((layers, rows, nf * w), BF16),
        in_specs=[pl.BlockSpec((nf, 1, rows, w), lambda l: (0, l, 0, 0))],
        out_specs=pl.BlockSpec((1, rows, nf * w), lambda l: (l, 0, 0)),
        name="join_columns",
    )(d)


def gram_kernel(pos_ref, s_ref, t_ref, o_ref):
    c = pos_ref[0]

    def block_row(i):
        a, b = s_ref[:, i * BLK :], t_ref[:, i * BLK :]
        return dotf(a[:, :BLK], a, 0, 0) + dotf(b[:, :BLK], b, 0, 0)

    def share(i, j):
        wi = s_ref.shape[1] - i * BLK
        o_ref[:, :wi] = block_row(i) * (1.0 / D)
        o_ref[:, wi:] = block_row(j) * (1.0 / D)

    @pl.when(c == 0)
    def _():
        share(0, 3)

    @pl.when(c != 0)
    def _():
        share(1, 2)


def gram_share(pos, s, t):
    return pl.pallas_call(
        gram_kernel,
        out_shape=jax.ShapeDtypeStruct((BLK, 5 * BLK), F32),
        in_specs=[SMEM_SPEC, VMEM_SPEC, VMEM_SPEC],
        name="gram",
    )(pos, s, t)


def factor_block(tiles, out_ref):
    nt = len(tiles)
    lane = lax.broadcasted_iota(jnp.int32, (VR, BLK), 1)
    sub = lax.broadcasted_iota(jnp.int32, (VR, BLK), 0)
    tiles = list(tiles)
    for b in range(nt):
        c = VR * b
        t = tiles[b]
        inblk = (lane >= c) & (lane < c + VR)
        cols = [jnp.broadcast_to(t[:, c + j : c + j + 1], (VR, BLK)) for j in range(VR)]
        e = [[jnp.broadcast_to(cols[j][i : i + 1, :], (VR, BLK)) if i >= j else None for j in range(VR)] for i in range(VR)]
        start = jnp.where(inblk, (lane - c == sub).astype(F32), t)
        rows = [jnp.broadcast_to(start[j : j + 1, :], (VR, BLK)) for j in range(VR)]
        m = [[None] * VR for _ in range(VR)]
        r = [None] * VR
        for j in range(VR):
            r[j] = 1.0 / e[j][j]
            for i in range(j + 1, VR):
                m[i][j] = e[i][j] * r[j]
            for i in range(j + 1, VR):
                for k in range(i, VR):
                    e[k][i] = e[k][i] - m[k][j] * e[i][j]
            for i in range(j + 1, VR):
                rows[i] = rows[i] - m[i][j] * rows[j]
        for j in range(VR):
            out_ref[c + j : c + j + 1, :] = (rows[j] * lax.rsqrt(e[j][j]))[0:1, :]
        for s in range(b + 1, nt):
            q = [jnp.broadcast_to(tiles[s][:, c + j : c + j + 1], (VR, BLK)) for j in range(VR)]
            acc = jnp.where(inblk, 0.0, tiles[s])
            for j in range(VR):
                for i in range(j + 1, VR):
                    q[i] = q[i] - q[j] * m[i][j]
                acc = acc - (q[j] * r[j]) * rows[j]
            tiles[s] = acc


def chol_kernel(pos_ref, ga_ref, gb_ref, s_ref, o_ref, t_ref, a_ref, x_ref, w_ref):
    c = pos_ref[0]
    n = a_ref.shape[0]
    nb = n // BLK

    def place(src, i, j):
        wi = n - i * BLK
        a_ref[i * BLK : (i + 1) * BLK, i * BLK :] = src[:, :wi]
        a_ref[j * BLK : (j + 1) * BLK, j * BLK :] = src[:, wi:]

    @pl.when(c == 0)
    def _():
        place(ga_ref, 0, 3)
        place(gb_ref, 1, 2)

    @pl.when(c != 0)
    def _():
        place(gb_ref, 0, 3)
        place(ga_ref, 1, 2)

    x_ref[...] = s_ref[...]
    row = lax.broadcasted_iota(jnp.int32, (BLK, BLK), 0)
    col = lax.broadcasted_iota(jnp.int32, (BLK, BLK), 1)
    t_ref[...] = jnp.zeros(t_ref.shape, F32)
    for ob in range(nb):
        lo = ob * BLK
        hi = lo + BLK
        factor_block([a_ref[lo + VR * i : lo + VR * i + VR, lo:hi] for i in range(BLK // VR)], w_ref)
        w = jnp.where(row >= col, w_ref[...], 0.0)
        xo = dotf(x_ref[:, lo:hi], w, 1, 1)
        t_ref[lo:hi, lo:hi] = (row == col).astype(F32)
        to = dotf(t_ref[:hi, lo:hi], w, 1, 1)
        if ob + 1 < nb:
            u = dotf(w, a_ref[lo:hi, hi:], 1, 0)
            for ib in range(ob + 1, nb):
                off = (ib - ob - 1) * BLK
                a_ref[ib * BLK : (ib + 1) * BLK, ib * BLK :] -= dotf(u[:, off : off + BLK], u[:, off:], 0, 0)
            x_ref[:, hi:] -= dotf(xo, u, 1, 0)
            t_ref[:hi, hi:] -= dotf(to, u, 1, 0)
        o_ref[:, lo:hi] = xo
        t_ref[:hi, lo:hi] = to


def chol_basis(pos, ga, gb, s):
    rows, n = s.shape
    return pl.pallas_call(
        chol_kernel,
        out_shape=(jax.ShapeDtypeStruct((rows, n), F32), jax.ShapeDtypeStruct((n, n), F32)),
        in_specs=[SMEM_SPEC, VMEM_SPEC, VMEM_SPEC, VMEM_SPEC],
        scratch_shapes=[pltpu.VMEM((n, n), F32), pltpu.VMEM((rows, n), F32), pltpu.VMEM((BLK, BLK), F32)],
        cost_estimate=pl.CostEstimate(flops=20_000_000_000, bytes_accessed=40_000_000, transcendentals=1024),
        name="cholesky_basis",
    )(pos, ga, gb, s)


CHUNKS = 8


def refresh_kernel(s_hbm, g_hbm, t_ref, m_ref, p_ref, d_hbm, s_buf, g_buf, q_buf, d_buf, u_buf, s_sem, g_sem, d_sem):
    size = s_buf.shape[0] // CHUNKS
    n = t_ref.shape[0]
    half = n // 2

    def part(ref, k):
        return ref.at[k * size : (k + 1) * size]

    s_copies = [pltpu.make_async_copy(part(s_hbm, k), part(s_buf, k), s_sem.at[k]) for k in range(CHUNKS)]
    g_copies = [pltpu.make_async_copy(part(g_hbm, k), part(g_buf, k), g_sem.at[k]) for k in range(CHUNKS)]
    d_copies = [pltpu.make_async_copy(part(d_buf, k), part(d_hbm, k), d_sem.at[k]) for k in range(CHUNKS)]
    for k in range(CHUNKS):
        s_copies[k].start()
        g_copies[k].start()
    t = t_ref[...]
    th = t.astype(BF16)
    tl = (t - th.astype(F32)).astype(BF16)
    total = None
    for k in range(CHUNKS):
        s_copies[k].wait()
        s = s_buf[k * size : (k + 1) * size, :]
        sh = s.astype(BF16)
        sl = (s - sh.astype(F32)).astype(BF16)

        def cols(lo, hi):
            return dotb(sh[:, :hi], th[:hi, lo:hi], 1, 0) + (
                dotb(sh[:, :hi], tl[:hi, lo:hi], 1, 0) + dotb(sl[:, :hi], th[:hi, lo:hi], 1, 0)
            )

        q = jnp.concatenate([cols(0, half), cols(half, n)], axis=1).astype(BF16)
        q_buf[k * size : (k + 1) * size, :] = q
        g_copies[k].wait()
        term = dotb(q, g_buf[k * size : (k + 1) * size, :], 0, 0)
        total = term if total is None else total + term
    projected = total * (1.0 / ROOT)
    share = p_ref.shape[1]
    for i in range(p_ref.shape[0]):
        pr = projected[i * share : (i + 1) * share, :]
        p_ref[i] = pr
        first = 0.9 * m_ref[i, 0] + 0.1 * pr
        second = 0.95 * m_ref[i, 1] + 0.05 * pr * pr
        u_buf[i * share : (i + 1) * share, :] = (first / (jnp.sqrt(second) + 1e-08)).astype(BF16)
    update = u_buf[...]
    for k in range(CHUNKS):
        d = dotb(q_buf[k * size : (k + 1) * size, :], update, 1, 0)
        d_buf[k * size : (k + 1) * size, :] = (d * (1.0 / ROOT)).astype(BF16)
        d_copies[k].start()
    for k in range(CHUNKS):
        d_copies[k].wait()


def refresh(s, g, t, moments):
    rows, n = s.shape
    w = g.shape[1]
    return pl.pallas_call(
        refresh_kernel,
        out_shape=(jax.ShapeDtypeStruct((NP, n // NP, w), F32), jax.ShapeDtypeStruct((rows, w), BF16)),
        in_specs=[ANY_SPEC, ANY_SPEC, VMEM_SPEC, VMEM_SPEC],
        out_specs=(VMEM_SPEC, ANY_SPEC),
        scratch_shapes=[
            pltpu.VMEM((rows, n), F32),
            pltpu.VMEM((rows, w), BF16),
            pltpu.VMEM((rows, n), BF16),
            pltpu.VMEM((rows, w), BF16),
            pltpu.VMEM((n, w), BF16),
            pltpu.SemaphoreType.DMA((CHUNKS,)),
            pltpu.SemaphoreType.DMA((CHUNKS,)),
            pltpu.SemaphoreType.DMA((CHUNKS,)),
        ],
        cost_estimate=pl.CostEstimate(flops=10_000_000_000, bytes_accessed=20_000_000, transcendentals=200_000),
        name="refresh",
    )(s, g, t, moments)


def per_device(gradients, test_matrix, first_moment, second_moment):
    layers, local_rows, col_width = gradients.shape
    rank = test_matrix.shape[1]
    c = lax.axis_index("fsdp") % NC
    pos = jnp.stack([c, c]).astype(jnp.int32)
    everyone = ("fsdp", "panel")

    sketches = jnp.dot(gradients.reshape(layers * local_rows, col_width), test_matrix, preferred_element_type=F32)
    sketches = jnp.pad(sketches.reshape(layers, local_rows, rank), ((0, NP - layers), (0, 0), (0, 0)))
    rows = exchange(sketches, "panel").reshape(NP * local_rows, rank)
    all_rows = lax.all_gather(rows, "fsdp", axis=0, tiled=True)

    share = gram_share(pos, rows, swap_core(rows)).reshape(NX * NZ, VR, 5 * BLK)
    share = jnp.sum(exchange(share, "fsdp", SAME_CORE), axis=0, keepdims=True)
    share = exchange(jnp.broadcast_to(share, (NX * NZ, VR, 5 * BLK)), "fsdp", SAME_CORE).reshape(BLK, 5 * BLK)

    blocks = exchange(cut_columns(gradients).reshape(NF * NP, local_rows, -1), everyone)
    width = blocks.shape[2]
    blocks = blocks.reshape(-1, width)
    moments = jnp.stack([first_moment, second_moment], axis=1)
    moments = exchange(jnp.pad(moments, ((0, NP - layers), (0, 0), (0, 0), (0, 0))), "panel")

    basis, inverse = chol_basis(pos, share, swap_core(share), rows)
    subspace = exchange(basis.reshape(NP, local_rows, rank), "panel")[:layers]
    projected, delta = refresh(all_rows, blocks, inverse, moments)
    delta = exchange(delta.reshape(NF * NP, local_rows, width), everyone)
    projected = exchange(projected, "panel")[:layers]
    new_first = 0.9 * first_moment + 0.1 * projected
    new_second = 0.95 * second_moment + 0.05 * projected * projected
    weight_delta = join_columns(delta.reshape(NF, NP, local_rows, width), layers)
    return (subspace, new_first, new_second, weight_delta)


def solution(mesh):
    return jax.shard_map(
        per_device,
        mesh=mesh,
        in_specs=(
            P(None, ("fsdp", "panel"), None),
            P(),
            P(None, "panel", "fsdp"),
            P(None, "panel", "fsdp"),
        ),
        out_specs=(
            P(None, ("fsdp", "panel"), None),
            P(None, "panel", "fsdp"),
            P(None, "panel", "fsdp"),
            P(None, ("fsdp", "panel"), None),
        ),
        check_vma=False,
    )
```

```python
import jax
import jax.numpy as jnp
from jax import lax
from jax.experimental import pallas as pl
from jax.experimental.pallas import tpu as pltpu
from jax.sharding import PartitionSpec as P


D = 4096
ROOT = 64.0
NX, NZ, NC, NP = 4, 4, 2, 4
NF = NX * NZ * NC
BLK, VR = 128, 8
HI = lax.Precision.HIGHEST
F32, BF16 = jnp.float32, jnp.bfloat16
SMEM_SPEC = pl.BlockSpec(memory_space=pltpu.SMEM)
VMEM_SPEC = pl.BlockSpec(memory_space=pltpu.VMEM)
ANY_SPEC = pl.BlockSpec(memory_space=pl.ANY)


SAME_CORE = [[NC * i + c for i in range(NX * NZ)] for c in range(NC)]


def swap_core(v):
    return lax.ppermute(v, "fsdp", [(f, f ^ 1) for f in range(NF)])


def shift_y(v, s, keep):
    pairs = [(p, (p + s) % NP) for p in range(NP)]
    return lax.ppermute(v, "panel", [pr for pr in pairs if keep(*pr)])


def rem(a, n):
    return lax.rem(a + n, n)


def exchange(v, axes, groups=None):
    return lax.all_to_all(v, axes, split_axis=0, concat_axis=0, tiled=True, axis_index_groups=groups)


def dotf(a, b, ca, cb):
    return lax.dot_general(a, b, (((ca,), (cb,)), ((), ())), precision=HI, preferred_element_type=F32)


def dotb(a, b, ca, cb):
    return lax.dot_general(a, b, (((ca,), (cb,)), ((), ())), preferred_element_type=F32)


def cut_kernel(g_ref, o_ref):
    w = o_ref.shape[3]
    for f in range(o_ref.shape[0]):
        o_ref[f, 0] = g_ref[0, :, f * w : (f + 1) * w]


def cut_columns(g):
    layers, rows, width = g.shape
    w = width // NF
    return pl.pallas_call(
        cut_kernel,
        grid=(layers,),
        out_shape=jax.ShapeDtypeStruct((NF, NP, rows, w), BF16),
        in_specs=[pl.BlockSpec((1, rows, width), lambda l: (l, 0, 0))],
        out_specs=pl.BlockSpec((NF, 1, rows, w), lambda l: (0, l, 0, 0)),
        name="cut_columns",
    )(g)


def join_kernel(d_ref, o_hbm, o_buf, sem):
    w = d_ref.shape[3]
    layers = o_buf.shape[0]
    copies = [pltpu.make_async_copy(o_buf.at[l], o_hbm.at[l], sem.at[l]) for l in range(layers)]
    for l in range(layers):
        for f in range(d_ref.shape[0]):
            o_buf[l, :, f * w : (f + 1) * w] = d_ref[f, l]
        copies[l].start()
    for l in range(layers):
        copies[l].wait()


def join_columns(d, layers):
    nf, _, rows, w = d.shape
    return pl.pallas_call(
        join_kernel,
        out_shape=jax.ShapeDtypeStruct((layers, rows, nf * w), BF16),
        in_specs=[VMEM_SPEC],
        out_specs=ANY_SPEC,
        scratch_shapes=[pltpu.VMEM((layers, rows, nf * w), BF16), pltpu.SemaphoreType.DMA((layers,))],
        compiler_params=pltpu.CompilerParams(vmem_limit_bytes=16 << 20),
        name="join_columns",
    )(d)


def pack_kernel(pos_ref, f_ref, s_ref, *outs):
    p = pos_ref[1]
    last = f_ref.shape[0] - 1
    for s in range(NP):
        l = jnp.minimum(rem(p + s, NP), last)
        outs[s][0] = f_ref[l]
        outs[s][1] = s_ref[l]


def pack_moments(pos, first, second):
    return pl.pallas_call(
        pack_kernel,
        out_shape=[jax.ShapeDtypeStruct((2, *first.shape[1:]), F32)] * NP,
        in_specs=[SMEM_SPEC, VMEM_SPEC, VMEM_SPEC],
        name="pack_moments",
    )(pos, first, second)


def gram_kernel(pos_ref, s_ref, t_ref, o_ref):
    c = pos_ref[0]

    def block_row(i):
        a, b = s_ref[:, i * BLK :], t_ref[:, i * BLK :]
        return dotf(a[:, :BLK], a, 0, 0) + dotf(b[:, :BLK], b, 0, 0)

    def share(i, j):
        wi = s_ref.shape[1] - i * BLK
        o_ref[:, :wi] = block_row(i) * (1.0 / D)
        o_ref[:, wi:] = block_row(j) * (1.0 / D)

    @pl.when(c == 0)
    def _():
        share(0, 3)

    @pl.when(c != 0)
    def _():
        share(1, 2)


def gram_share(pos, s, t):
    return pl.pallas_call(
        gram_kernel,
        out_shape=jax.ShapeDtypeStruct((BLK, 5 * BLK), F32),
        in_specs=[SMEM_SPEC, VMEM_SPEC, VMEM_SPEC],
        name="gram",
    )(pos, s, t)


def factor_block(tiles, out_ref):
    nt = len(tiles)
    lane = lax.broadcasted_iota(jnp.int32, (VR, BLK), 1)
    sub = lax.broadcasted_iota(jnp.int32, (VR, BLK), 0)
    tiles = list(tiles)
    for b in range(nt):
        c = VR * b
        t = tiles[b]
        inblk = (lane >= c) & (lane < c + VR)
        cols = [jnp.broadcast_to(t[:, c + j : c + j + 1], (VR, BLK)) for j in range(VR)]
        e = [[jnp.broadcast_to(cols[j][i : i + 1, :], (VR, BLK)) if i >= j else None for j in range(VR)] for i in range(VR)]
        start = jnp.where(inblk, (lane - c == sub).astype(F32), t)
        rows = [jnp.broadcast_to(start[j : j + 1, :], (VR, BLK)) for j in range(VR)]
        m = [[None] * VR for _ in range(VR)]
        r = [None] * VR
        for j in range(VR):
            r[j] = 1.0 / e[j][j]
            for i in range(j + 1, VR):
                m[i][j] = e[i][j] * r[j]
            for i in range(j + 1, VR):
                for k in range(i, VR):
                    e[k][i] = e[k][i] - m[k][j] * e[i][j]
            for i in range(j + 1, VR):
                rows[i] = rows[i] - m[i][j] * rows[j]
        for j in range(VR):
            out_ref[c + j : c + j + 1, :] = (rows[j] * lax.rsqrt(e[j][j]))[0:1, :]
        scaled = [rows[j] * r[j] for j in range(VR)]
        solved = list(scaled)
        for j in reversed(range(VR)):
            for i in range(j):
                solved[i] = solved[i] - m[j][i] * solved[j]
        for s in range(b + 1, nt):
            q = [jnp.broadcast_to(tiles[s][:, c + j : c + j + 1], (VR, BLK)) for j in range(VR)]
            acc = jnp.where(inblk, 0.0, tiles[s])
            for j in range(VR):
                if s == b + 1:
                    for i in range(j + 1, VR):
                        q[i] = q[i] - q[j] * m[i][j]
                    acc = acc - q[j] * scaled[j]
                else:
                    acc = acc - q[j] * solved[j]
            tiles[s] = acc


def chol_kernel(pos_ref, ga_ref, gb_ref, s_ref, o_ref, t_ref, a_ref, x_ref, w_ref):
    c, p = pos_ref[0], pos_ref[1]
    n = a_ref.shape[0]
    nb = n // BLK
    rows = o_ref.shape[1]

    def place(src, i, j):
        wi = n - i * BLK
        a_ref[i * BLK : (i + 1) * BLK, i * BLK :] = src[:, :wi]
        a_ref[j * BLK : (j + 1) * BLK, j * BLK :] = src[:, wi:]

    @pl.when(c == 0)
    def _():
        place(ga_ref, 0, 3)
        place(gb_ref, 1, 2)

    @pl.when(c != 0)
    def _():
        place(gb_ref, 0, 3)
        place(ga_ref, 1, 2)

    x_ref[...] = s_ref[...]
    row = lax.broadcasted_iota(jnp.int32, (BLK, BLK), 0)
    col = lax.broadcasted_iota(jnp.int32, (BLK, BLK), 1)
    t_ref[...] = jnp.zeros(t_ref.shape, F32)
    for ob in range(nb):
        lo = ob * BLK
        hi = lo + BLK
        factor_block([a_ref[lo + VR * i : lo + VR * i + VR, lo:hi] for i in range(BLK // VR)], w_ref)
        w = jnp.where(row >= col, w_ref[...], 0.0)
        xo = dotf(x_ref[:, lo:hi], w, 1, 1)
        t_ref[lo:hi, lo:hi] = (row == col).astype(F32)
        to = dotf(t_ref[:hi, lo:hi], w, 1, 1)
        if ob + 1 < nb:
            u = dotf(w, a_ref[lo:hi, hi:], 1, 0)
            for ib in range(ob + 1, nb):
                off = (ib - ob - 1) * BLK
                a_ref[ib * BLK : (ib + 1) * BLK, ib * BLK :] -= dotf(u[:, off : off + BLK], u[:, off:], 0, 0)
            x_ref[:, hi:] -= dotf(xo, u, 1, 0)
            t_ref[:hi, hi:] -= dotf(to, u, 1, 0)
        for k in range(NP):
            o_ref[rem(p - k, NP), :, lo:hi] = xo[k * rows : (k + 1) * rows, :]
        t_ref[:hi, lo:hi] = to


def chol_basis(pos, ga, gb, s):
    rows, n = s.shape
    return pl.pallas_call(
        chol_kernel,
        out_shape=(jax.ShapeDtypeStruct((NP, rows // NP, n), F32), jax.ShapeDtypeStruct((n, n), F32)),
        in_specs=[SMEM_SPEC, VMEM_SPEC, VMEM_SPEC, VMEM_SPEC],
        scratch_shapes=[pltpu.VMEM((n, n), F32), pltpu.VMEM((rows, n), F32), pltpu.VMEM((BLK, BLK), F32)],
        cost_estimate=pl.CostEstimate(flops=20_000_000_000, bytes_accessed=40_000_000, transcendentals=1024),
        name="cholesky_basis",
    )(pos, ga, gb, s)


CHUNKS = 4


def chunk(k, size):
    return pl.ds(pl.multiple_of(k * size, size), size)


def basis_kernel(s_hbm, t_ref, q_hbm, s_buf, q_buf, s_sem, q_sem):
    size = s_buf.shape[0] // CHUNKS

    def load(k):
        return pltpu.make_async_copy(s_hbm.at[chunk(k, size)], s_buf.at[chunk(k, size)], s_sem.at[k])

    def store(k):
        return pltpu.make_async_copy(q_buf.at[chunk(k, size)], q_hbm.at[chunk(k, size)], q_sem.at[k])

    def start(k, carry):
        load(k).start()
        return carry

    lax.fori_loop(0, CHUNKS, start, 0)
    t = t_ref[...]
    th = t.astype(BF16)
    tl = (t - th.astype(F32)).astype(BF16)

    def step(k, carry):
        load(k).wait()
        s = s_buf[chunk(k, size), :]
        sh = s.astype(BF16)
        sl = (s - sh.astype(F32)).astype(BF16)
        q = dotb(sh, th, 1, 0) + (dotb(sh, tl, 1, 0) + dotb(sl, th, 1, 0))
        q_buf[chunk(k, size), :] = q.astype(BF16)
        store(k).start()
        return carry

    lax.fori_loop(0, CHUNKS, step, 0)

    def finish(k, carry):
        store(k).wait()
        return carry

    lax.fori_loop(0, CHUNKS, finish, 0)


def basis_rows(s, t):
    rows, n = s.shape
    return pl.pallas_call(
        basis_kernel,
        out_shape=jax.ShapeDtypeStruct((rows, n), BF16),
        in_specs=[ANY_SPEC, VMEM_SPEC],
        out_specs=ANY_SPEC,
        scratch_shapes=[
            pltpu.VMEM((rows, n), F32),
            pltpu.VMEM((rows, n), BF16),
            pltpu.SemaphoreType.DMA((CHUNKS,)),
            pltpu.SemaphoreType.DMA((CHUNKS,)),
        ],
        cost_estimate=pl.CostEstimate(flops=5_000_000_000, bytes_accessed=12_000_000, transcendentals=0),
        name="basis_rows",
    )(s, t)


PARTS = 2


def refresh_kernel(
    pos_ref, q0_hbm, q1_hbm, g_hbm, m0_ref, m1_ref, m2_ref, m3_ref, p_ref, d_hbm, q_buf, g_buf, d_buf, pt_ref, u_ref, q_sem, g_sem, d_sem
):
    c, p = pos_ref[0], pos_ref[1]
    share = p_ref.shape[2]
    chips, rows, w = g_buf.shape[1:]
    n = q_buf.shape[3]
    size = chips // PARTS
    loads, stores, places = [], [], []
    for h, q_hbm in enumerate((q0_hbm, q1_hbm)):
        core = c if h == 0 else 1 - c
        for k in range(PARTS):
            part = pl.ds(k * size, size)
            i = h * PARTS + k
            loads.append(pltpu.make_async_copy(q_hbm.at[part], q_buf.at[h, part], q_sem.at[i]))
            loads.append(pltpu.make_async_copy(g_hbm.at[part, core], g_buf.at[h, part], g_sem.at[i]))
            stores.append(pltpu.make_async_copy(d_buf.at[h, part], d_hbm.at[part, core], d_sem.at[i]))
            places.append((h, k * size, (k + 1) * size))
    for copy in loads:
        copy.start()
    pt = None
    for i, (h, lo, hi) in enumerate(places):
        loads[2 * i].wait()
        loads[2 * i + 1].wait()
        term = dotb(g_buf[h, lo:hi].reshape(size * rows, w), q_buf[h, lo:hi].reshape(size * rows, n), 0, 0)
        pt = term if pt is None else pt + term
    pt = pt * (1.0 / ROOT)
    for i in range(NP):
        pt_ref[i] = pt[:, i * share : (i + 1) * share]
    for s, m_ref in enumerate((m0_ref, m1_ref, m2_ref, m3_ref)):
        i = rem(p - s, NP)
        pr = pt_ref[i]
        p_ref[s] = pr.astype(BF16)
        first = 0.9 * m_ref[0] + 0.1 * pr
        second = 0.95 * m_ref[1] + 0.05 * pr * pr
        u_ref[i] = (first / (jnp.sqrt(second) + 1e-08)).astype(BF16)
    update = jnp.concatenate([u_ref[i] for i in range(NP)], axis=1)
    for i, (h, lo, hi) in enumerate(places):
        d = dotb(q_buf[h, lo:hi].reshape(size * rows, n), update, 1, 1)
        d_buf[h, lo:hi] = (d * (1.0 / ROOT)).astype(BF16).reshape(size, rows, w)
        stores[i].start()
    for copy in stores:
        copy.wait()


def refresh(pos, q0, q1, g, moments):
    chips, rows, n = q0.shape
    w = g.shape[3]
    share = n // NP
    return pl.pallas_call(
        refresh_kernel,
        out_shape=(jax.ShapeDtypeStruct((NP, w, share), BF16), jax.ShapeDtypeStruct(g.shape, BF16)),
        in_specs=[SMEM_SPEC, ANY_SPEC, ANY_SPEC, ANY_SPEC] + [VMEM_SPEC] * NP,
        out_specs=(VMEM_SPEC, ANY_SPEC),
        scratch_shapes=[
            pltpu.VMEM((NC, chips, rows, n), BF16),
            pltpu.VMEM((NC, chips, rows, w), BF16),
            pltpu.VMEM((NC, chips, rows, w), BF16),
            pltpu.VMEM((NP, w, share), F32),
            pltpu.VMEM((NP, w, share), BF16),
            pltpu.SemaphoreType.DMA((NC * PARTS,)),
            pltpu.SemaphoreType.DMA((NC * PARTS,)),
            pltpu.SemaphoreType.DMA((NC * PARTS,)),
        ],
        cost_estimate=pl.CostEstimate(flops=6_000_000_000, bytes_accessed=12_000_000, transcendentals=200_000),
        name="refresh",
    )(pos, q0, q1, g, *moments)


def per_device(gradients, test_matrix, first_moment, second_moment):
    layers, local_rows, col_width = gradients.shape
    rank = test_matrix.shape[1]
    c = lax.axis_index("fsdp") % NC
    p = lax.axis_index("panel")
    pos = jnp.stack([c, p]).astype(jnp.int32)
    everyone = ("fsdp", "panel")

    def into(src, dst):
        return dst < layers

    def back(src, dst):
        return src < layers

    def returned(slots):
        slots = jnp.stack([slots[0]] + [shift_y(slots[s], NP - s, back) for s in range(1, NP)])
        return jnp.stack([lax.dynamic_index_in_dim(slots, rem(l - p, NP), 0, keepdims=False) for l in range(layers)])

    sketches = jnp.dot(gradients.reshape(layers * local_rows, col_width), test_matrix, preferred_element_type=F32)
    sketches = jnp.pad(sketches.reshape(layers, local_rows, rank), ((0, NP - layers), (0, 0), (0, 0)))
    rows = exchange(sketches, "panel").reshape(NP * local_rows, rank)
    core_rows = lax.all_gather(rows, "fsdp", axis=0, tiled=True, axis_index_groups=SAME_CORE)

    first_t, second_t = jnp.swapaxes(first_moment, 1, 2), jnp.swapaxes(second_moment, 1, 2)
    moments = pack_moments(pos, first_t, second_t)
    moments = [moments[0]] + [shift_y(moments[s], s, into) for s in range(1, NP)]

    share = gram_share(pos, rows, swap_core(rows)).reshape(NX * NZ, VR, 5 * BLK)
    share = exchange(share, "fsdp", SAME_CORE)
    share = jnp.sum(share, axis=0, keepdims=True)
    share = exchange(jnp.broadcast_to(share, (NX * NZ, VR, 5 * BLK)), "fsdp", SAME_CORE)
    share = share.reshape(BLK, 5 * BLK)

    blocks = cut_columns(gradients)
    blocks = exchange(blocks.reshape(NF * NP, local_rows, -1), everyone)
    width = blocks.shape[2]

    basis, inverse = chol_basis(pos, share, swap_core(share), rows)
    subspace = returned(basis)
    q = basis_rows(core_rows, inverse)
    q_other = swap_core(q)
    chips = (NX * NZ, NP * local_rows, rank)
    blocks = blocks.reshape(NX * NZ, NC, NP * local_rows, width)
    projected, delta = refresh(pos, q.reshape(chips), q_other.reshape(chips), blocks, moments)
    delta = exchange(delta.reshape(NF * NP, local_rows, width), everyone)
    projected = returned(projected).astype(F32)
    new_first = 0.9 * first_t + 0.1 * projected
    new_second = 0.95 * second_t + 0.05 * projected * projected
    weight_delta = join_columns(delta.reshape(NF, NP, local_rows, width), layers)
    return (subspace, jnp.swapaxes(new_first, 1, 2), jnp.swapaxes(new_second, 1, 2), weight_delta)


def solution(mesh):
    return jax.shard_map(
        per_device,
        mesh=mesh,
        in_specs=(
            P(None, ("fsdp", "panel"), None),
            P(),
            P(None, "panel", "fsdp"),
            P(None, "panel", "fsdp"),
        ),
        out_specs=(
            P(None, ("fsdp", "panel"), None),
            P(None, "panel", "fsdp"),
            P(None, "panel", "fsdp"),
            P(None, ("fsdp", "panel"), None),
        ),
        check_vma=False,
    )
```

```python
import jax
import jax.numpy as jnp
from jax import lax
from jax.experimental import pallas as pl
from jax.experimental.pallas import tpu as pltpu
from jax.sharding import PartitionSpec as P


D = 4096
ROOT = 64.0
NX, NZ, NC, NP = 4, 4, 2, 4
NF = NX * NZ * NC
BLK, VR = 128, 8
HI = lax.Precision.HIGHEST
F32, BF16 = jnp.float32, jnp.bfloat16
SMEM_SPEC = pl.BlockSpec(memory_space=pltpu.SMEM)
VMEM_SPEC = pl.BlockSpec(memory_space=pltpu.VMEM)
ANY_SPEC = pl.BlockSpec(memory_space=pl.ANY)


SAME_CORE = [[NC * i + c for i in range(NX * NZ)] for c in range(NC)]


def swap_core(v):
    return lax.ppermute(v, "fsdp", [(f, f ^ 1) for f in range(NF)])


def shift_y(v, s, keep):
    pairs = [(p, (p + s) % NP) for p in range(NP)]
    return lax.ppermute(v, "panel", [pr for pr in pairs if keep(*pr)])


def rem(a, n):
    return lax.rem(a + n, n)


def exchange(v, axes, groups=None):
    return lax.all_to_all(v, axes, split_axis=0, concat_axis=0, tiled=True, axis_index_groups=groups)


def dotf(a, b, ca, cb):
    return lax.dot_general(a, b, (((ca,), (cb,)), ((), ())), precision=HI, preferred_element_type=F32)


def dotb(a, b, ca, cb):
    return lax.dot_general(a, b, (((ca,), (cb,)), ((), ())), preferred_element_type=F32)


def cut_kernel(g_ref, o_ref):
    w = o_ref.shape[3]
    for f in range(o_ref.shape[0]):
        o_ref[f, 0] = g_ref[0, :, f * w : (f + 1) * w]


def cut_columns(g):
    layers, rows, width = g.shape
    w = width // NF
    return pl.pallas_call(
        cut_kernel,
        grid=(layers,),
        out_shape=jax.ShapeDtypeStruct((NF, NP, rows, w), BF16),
        in_specs=[pl.BlockSpec((1, rows, width), lambda l: (l, 0, 0))],
        out_specs=pl.BlockSpec((NF, 1, rows, w), lambda l: (0, l, 0, 0)),
        name="cut_columns",
    )(g)


def join_kernel(d_ref, o_hbm, o_buf, sem):
    w = d_ref.shape[3]
    layers = o_buf.shape[0]
    copies = [pltpu.make_async_copy(o_buf.at[l], o_hbm.at[l], sem.at[l]) for l in range(layers)]
    for l in range(layers):
        for f in range(d_ref.shape[0]):
            o_buf[l, :, f * w : (f + 1) * w] = d_ref[f, l]
        copies[l].start()
    for l in range(layers):
        copies[l].wait()


def join_columns(d, layers):
    nf, _, rows, w = d.shape
    return pl.pallas_call(
        join_kernel,
        out_shape=jax.ShapeDtypeStruct((layers, rows, nf * w), BF16),
        in_specs=[VMEM_SPEC],
        out_specs=ANY_SPEC,
        scratch_shapes=[pltpu.VMEM((layers, rows, nf * w), BF16), pltpu.SemaphoreType.DMA((layers,))],
        compiler_params=pltpu.CompilerParams(vmem_limit_bytes=16 << 20),
        name="join_columns",
    )(d)


def pack_kernel(pos_ref, f_ref, s_ref, *outs):
    p = pos_ref[1]
    last = f_ref.shape[0] - 1
    for s in range(NP):
        l = jnp.minimum(rem(p + s, NP), last)
        outs[s][0] = f_ref[l]
        outs[s][1] = s_ref[l]


def pack_moments(pos, first, second):
    return pl.pallas_call(
        pack_kernel,
        out_shape=[jax.ShapeDtypeStruct((2, *first.shape[1:]), F32)] * NP,
        in_specs=[SMEM_SPEC, VMEM_SPEC, VMEM_SPEC],
        name="pack_moments",
    )(pos, first, second)


def gram_kernel(pos_ref, s_ref, t_ref, o_ref):
    c = pos_ref[0]

    def block_row(i):
        a, b = s_ref[:, i * BLK :], t_ref[:, i * BLK :]
        return dotf(a[:, :BLK], a, 0, 0) + dotf(b[:, :BLK], b, 0, 0)

    def share(i, j):
        wi = s_ref.shape[1] - i * BLK
        o_ref[:, :wi] = block_row(i) * (1.0 / D)
        o_ref[:, wi:] = block_row(j) * (1.0 / D)

    @pl.when(c == 0)
    def _():
        share(0, 3)

    @pl.when(c != 0)
    def _():
        share(1, 2)


def gram_share(pos, s, t):
    return pl.pallas_call(
        gram_kernel,
        out_shape=jax.ShapeDtypeStruct((BLK, 5 * BLK), F32),
        in_specs=[SMEM_SPEC, VMEM_SPEC, VMEM_SPEC],
        name="gram",
    )(pos, s, t)


def factor_block(tiles, out_ref):
    nt = len(tiles)
    lane = lax.broadcasted_iota(jnp.int32, (VR, BLK), 1)
    sub = lax.broadcasted_iota(jnp.int32, (VR, BLK), 0)
    tiles = list(tiles)
    for b in range(nt):
        c = VR * b
        t = tiles[b]
        inblk = (lane >= c) & (lane < c + VR)
        cols = [jnp.broadcast_to(t[:, c + j : c + j + 1], (VR, BLK)) for j in range(VR)]
        e = [[jnp.broadcast_to(cols[j][i : i + 1, :], (VR, BLK)) if i >= j else None for j in range(VR)] for i in range(VR)]
        start = jnp.where(inblk, (lane - c == sub).astype(F32), t)
        rows = [jnp.broadcast_to(start[j : j + 1, :], (VR, BLK)) for j in range(VR)]
        m = [[None] * VR for _ in range(VR)]
        r = [None] * VR
        for j in range(VR):
            r[j] = 1.0 / e[j][j]
            for i in range(j + 1, VR):
                m[i][j] = e[i][j] * r[j]
            for i in range(j + 1, VR):
                for k in range(i, VR):
                    e[k][i] = e[k][i] - m[k][j] * e[i][j]
            for i in range(j + 1, VR):
                rows[i] = rows[i] - m[i][j] * rows[j]
        for j in range(VR):
            out_ref[c + j : c + j + 1, :] = (rows[j] * lax.rsqrt(e[j][j]))[0:1, :]
        scaled = [rows[j] * r[j] for j in range(VR)]
        solved = list(scaled)
        for j in reversed(range(VR)):
            for i in range(j):
                solved[i] = solved[i] - m[j][i] * solved[j]
        for s in range(b + 1, nt):
            q = [jnp.broadcast_to(tiles[s][:, c + j : c + j + 1], (VR, BLK)) for j in range(VR)]
            acc = jnp.where(inblk, 0.0, tiles[s])
            for j in range(VR):
                if s == b + 1:
                    for i in range(j + 1, VR):
                        q[i] = q[i] - q[j] * m[i][j]
                    acc = acc - q[j] * scaled[j]
                else:
                    acc = acc - q[j] * solved[j]
            tiles[s] = acc


def chol_kernel(pos_ref, ga_ref, gb_ref, s_ref, o0_ref, o1_ref, o2_ref, o3_ref, t_ref, a_ref, x_ref, w_ref, o_ref):
    c, p = pos_ref[0], pos_ref[1]
    n = a_ref.shape[0]
    nb = n // BLK
    rows = o_ref.shape[1]

    def place(src, i, j):
        wi = n - i * BLK
        a_ref[i * BLK : (i + 1) * BLK, i * BLK :] = src[:, :wi]
        a_ref[j * BLK : (j + 1) * BLK, j * BLK :] = src[:, wi:]

    @pl.when(c == 0)
    def _():
        place(ga_ref, 0, 3)
        place(gb_ref, 1, 2)

    @pl.when(c != 0)
    def _():
        place(gb_ref, 0, 3)
        place(ga_ref, 1, 2)

    x_ref[...] = s_ref[...]
    row = lax.broadcasted_iota(jnp.int32, (BLK, BLK), 0)
    col = lax.broadcasted_iota(jnp.int32, (BLK, BLK), 1)
    t_ref[...] = jnp.zeros(t_ref.shape, F32)
    for ob in range(nb):
        lo = ob * BLK
        hi = lo + BLK
        factor_block([a_ref[lo + VR * i : lo + VR * i + VR, lo:hi] for i in range(BLK // VR)], w_ref)
        w = jnp.where(row >= col, w_ref[...], 0.0)
        xo = dotf(x_ref[:, lo:hi], w, 1, 1)
        t_ref[lo:hi, lo:hi] = (row == col).astype(F32)
        to = dotf(t_ref[:hi, lo:hi], w, 1, 1)
        if ob + 1 < nb:
            u = dotf(w, a_ref[lo:hi, hi:], 1, 0)
            for ib in range(ob + 1, nb):
                off = (ib - ob - 1) * BLK
                a_ref[ib * BLK : (ib + 1) * BLK, ib * BLK :] -= dotf(u[:, off : off + BLK], u[:, off:], 0, 0)
            x_ref[:, hi:] -= dotf(xo, u, 1, 0)
            t_ref[:hi, hi:] -= dotf(to, u, 1, 0)
        for k in range(NP):
            o_ref[rem(p - k, NP), :, lo:hi] = xo[k * rows : (k + 1) * rows, :]
        t_ref[:hi, lo:hi] = to
    for k, ref in enumerate((o0_ref, o1_ref, o2_ref, o3_ref)):
        ref[...] = o_ref[k]


def chol_basis(pos, ga, gb, s):
    rows, n = s.shape
    return pl.pallas_call(
        chol_kernel,
        out_shape=[jax.ShapeDtypeStruct((rows // NP, n), F32)] * NP + [jax.ShapeDtypeStruct((n, n), F32)],
        in_specs=[SMEM_SPEC, VMEM_SPEC, VMEM_SPEC, VMEM_SPEC],
        scratch_shapes=[
            pltpu.VMEM((n, n), F32),
            pltpu.VMEM((rows, n), F32),
            pltpu.VMEM((BLK, BLK), F32),
            pltpu.VMEM((NP, rows // NP, n), F32),
        ],
        cost_estimate=pl.CostEstimate(flops=20_000_000_000, bytes_accessed=40_000_000, transcendentals=1024),
        name="cholesky_basis",
    )(pos, ga, gb, s)


CHUNKS = 4


def chunk(k, size):
    return pl.ds(pl.multiple_of(k * size, size), size)


def basis_kernel(s_hbm, t_ref, q_hbm, s_buf, q_buf, s_sem, q_sem):
    size = s_buf.shape[0] // CHUNKS

    def load(k):
        return pltpu.make_async_copy(s_hbm.at[chunk(k, size)], s_buf.at[chunk(k, size)], s_sem.at[k])

    def store(k):
        return pltpu.make_async_copy(q_buf.at[chunk(k, size)], q_hbm.at[chunk(k, size)], q_sem.at[k])

    def start(k, carry):
        load(k).start()
        return carry

    lax.fori_loop(0, CHUNKS, start, 0)
    t = t_ref[...]
    th = t.astype(BF16)
    tl = (t - th.astype(F32)).astype(BF16)

    def step(k, carry):
        load(k).wait()
        s = s_buf[chunk(k, size), :]
        sh = s.astype(BF16)
        sl = (s - sh.astype(F32)).astype(BF16)
        q = dotb(sh, th, 1, 0) + (dotb(sh, tl, 1, 0) + dotb(sl, th, 1, 0))
        q_buf[chunk(k, size), :] = q.astype(BF16)
        store(k).start()
        return carry

    lax.fori_loop(0, CHUNKS, step, 0)

    def finish(k, carry):
        store(k).wait()
        return carry

    lax.fori_loop(0, CHUNKS, finish, 0)


def basis_rows(s, t):
    rows, n = s.shape
    return pl.pallas_call(
        basis_kernel,
        out_shape=jax.ShapeDtypeStruct((rows, n), BF16),
        in_specs=[ANY_SPEC, VMEM_SPEC],
        out_specs=ANY_SPEC,
        scratch_shapes=[
            pltpu.VMEM((rows, n), F32),
            pltpu.VMEM((rows, n), BF16),
            pltpu.SemaphoreType.DMA((CHUNKS,)),
            pltpu.SemaphoreType.DMA((CHUNKS,)),
        ],
        cost_estimate=pl.CostEstimate(flops=5_000_000_000, bytes_accessed=12_000_000, transcendentals=0),
        name="basis_rows",
    )(s, t)


PARTS = 2


def refresh_kernel(
    pos_ref, q0_hbm, q1_hbm, g_hbm, m0_ref, m1_ref, m2_ref, m3_ref, p0_ref, p1_ref, p2_ref, p3_ref, d_hbm, q_buf, g_buf, d_buf, pt_ref, u_ref, q_sem, g_sem, d_sem
):
    c, p = pos_ref[0], pos_ref[1]
    outs = (p0_ref, p1_ref, p2_ref, p3_ref)
    share = p0_ref.shape[1]
    chips, rows, w = g_buf.shape[1:]
    n = q_buf.shape[3]
    size = chips // PARTS
    loads, stores, places = [], [], []
    for h, q_hbm in enumerate((q0_hbm, q1_hbm)):
        core = c if h == 0 else 1 - c
        for k in range(PARTS):
            part = pl.ds(k * size, size)
            i = h * PARTS + k
            loads.append(pltpu.make_async_copy(q_hbm.at[part], q_buf.at[h, part], q_sem.at[i]))
            loads.append(pltpu.make_async_copy(g_hbm.at[part, core], g_buf.at[h, part], g_sem.at[i]))
            stores.append(pltpu.make_async_copy(d_buf.at[h, part], d_hbm.at[part, core], d_sem.at[i]))
            places.append((h, k * size, (k + 1) * size))
    for copy in loads:
        copy.start()
    pt = None
    for i, (h, lo, hi) in enumerate(places):
        loads[2 * i].wait()
        loads[2 * i + 1].wait()
        term = dotb(g_buf[h, lo:hi].reshape(size * rows, w), q_buf[h, lo:hi].reshape(size * rows, n), 0, 0)
        pt = term if pt is None else pt + term
    pt = pt * (1.0 / ROOT)
    for i in range(NP):
        pt_ref[i] = pt[:, i * share : (i + 1) * share]
    for s, m_ref in enumerate((m0_ref, m1_ref, m2_ref, m3_ref)):
        i = rem(p - s, NP)
        pr = pt_ref[i]
        outs[s][...] = pr.astype(BF16)
        first = 0.9 * m_ref[0] + 0.1 * pr
        second = 0.95 * m_ref[1] + 0.05 * pr * pr
        u_ref[i] = (first / (jnp.sqrt(second) + 1e-08)).astype(BF16)
    update = jnp.concatenate([u_ref[i] for i in range(NP)], axis=1)
    for i, (h, lo, hi) in enumerate(places):
        d = dotb(q_buf[h, lo:hi].reshape(size * rows, n), update, 1, 1)
        d_buf[h, lo:hi] = (d * (1.0 / ROOT)).astype(BF16).reshape(size, rows, w)
        stores[i].start()
    for copy in stores:
        copy.wait()


def refresh(pos, q0, q1, g, moments):
    chips, rows, n = q0.shape
    w = g.shape[3]
    share = n // NP
    return pl.pallas_call(
        refresh_kernel,
        out_shape=[jax.ShapeDtypeStruct((w, share), BF16)] * NP + [jax.ShapeDtypeStruct(g.shape, BF16)],
        in_specs=[SMEM_SPEC, ANY_SPEC, ANY_SPEC, ANY_SPEC] + [VMEM_SPEC] * NP,
        out_specs=[VMEM_SPEC] * NP + [ANY_SPEC],
        scratch_shapes=[
            pltpu.VMEM((NC, chips, rows, n), BF16),
            pltpu.VMEM((NC, chips, rows, w), BF16),
            pltpu.VMEM((NC, chips, rows, w), BF16),
            pltpu.VMEM((NP, w, share), F32),
            pltpu.VMEM((NP, w, share), BF16),
            pltpu.SemaphoreType.DMA((NC * PARTS,)),
            pltpu.SemaphoreType.DMA((NC * PARTS,)),
            pltpu.SemaphoreType.DMA((NC * PARTS,)),
        ],
        cost_estimate=pl.CostEstimate(flops=6_000_000_000, bytes_accessed=12_000_000, transcendentals=200_000),
        name="refresh",
    )(pos, q0, q1, g, *moments)


def finish_kernel(pos_ref, r0_ref, r1_ref, r2_ref, r3_ref, m_ref, v_ref, first_ref, second_ref, r_buf):
    p = pos_ref[1]
    for s, ref in enumerate((r0_ref, r1_ref, r2_ref, r3_ref)):
        r_buf[s] = ref[...]
    for l in range(m_ref.shape[0]):
        pr = r_buf[rem(l - p, NP)].astype(F32)
        first_ref[l] = 0.9 * m_ref[l] + 0.1 * pr
        second_ref[l] = 0.95 * v_ref[l] + 0.05 * pr * pr


def finish_moments(pos, slots, first, second):
    shape = jax.ShapeDtypeStruct(first.shape, F32)
    return pl.pallas_call(
        finish_kernel,
        out_shape=(shape, shape),
        in_specs=[SMEM_SPEC] + [VMEM_SPEC] * (NP + 2),
        scratch_shapes=[pltpu.VMEM((NP, *slots[0].shape), BF16)],
        name="finish_moments",
    )(pos, *slots, first, second)


def per_device(gradients, test_matrix, first_moment, second_moment):
    layers, local_rows, col_width = gradients.shape
    rank = test_matrix.shape[1]
    c = lax.axis_index("fsdp") % NC
    p = lax.axis_index("panel")
    pos = jnp.stack([c, p]).astype(jnp.int32)
    everyone = ("fsdp", "panel")

    def into(src, dst):
        return dst < layers

    def back(src, dst):
        return src < layers

    def returned(slots):
        return [slots[0]] + [shift_y(slots[s], NP - s, back) for s in range(1, NP)]

    sketches = jnp.dot(gradients.reshape(layers * local_rows, col_width), test_matrix, preferred_element_type=F32)
    sketches = jnp.pad(sketches.reshape(layers, local_rows, rank), ((0, NP - layers), (0, 0), (0, 0)))
    rows = exchange(sketches, "panel").reshape(NP * local_rows, rank)
    core_rows = lax.all_gather(rows, "fsdp", axis=0, tiled=True, axis_index_groups=SAME_CORE)

    first_t, second_t = jnp.swapaxes(first_moment, 1, 2), jnp.swapaxes(second_moment, 1, 2)
    moments = pack_moments(pos, first_t, second_t)
    moments = [moments[0]] + [shift_y(moments[s], s, into) for s in range(1, NP)]

    share = gram_share(pos, rows, swap_core(rows)).reshape(NX * NZ, VR, 5 * BLK)
    share = exchange(share, "fsdp", SAME_CORE)
    share = jnp.sum(share, axis=0, keepdims=True)
    share = exchange(jnp.broadcast_to(share, (NX * NZ, VR, 5 * BLK)), "fsdp", SAME_CORE)
    share = share.reshape(BLK, 5 * BLK)

    blocks = cut_columns(gradients)
    width = blocks.shape[3]
    blocks = exchange(blocks.reshape(NF * NP, local_rows, width), everyone)

    other_share = swap_core(share)
    *basis, inverse = chol_basis(pos, share, other_share, rows)
    basis = returned(basis)
    q = basis_rows(core_rows, inverse)
    chips = (NX * NZ, NP * local_rows, rank)
    blocks = blocks.reshape(NX * NZ, NC, NP * local_rows, width)
    other_q = swap_core(q)
    *projected, delta = refresh(pos, q.reshape(chips), other_q.reshape(chips), blocks, moments)
    delta = exchange(delta.reshape(NF * NP, local_rows, width), everyone)
    projected = returned(projected)
    new_first, new_second = finish_moments(pos, projected, first_t, second_t)
    basis = jnp.stack(basis)
    subspace = jnp.stack([lax.dynamic_index_in_dim(basis, rem(l - p, NP), 0, keepdims=False) for l in range(layers)])
    weight_delta = join_columns(delta.reshape(NF, NP, local_rows, width), layers)
    return (subspace, jnp.swapaxes(new_first, 1, 2), jnp.swapaxes(new_second, 1, 2), weight_delta)


def solution(mesh):
    return jax.shard_map(
        per_device,
        mesh=mesh,
        in_specs=(
            P(None, ("fsdp", "panel"), None),
            P(),
            P(None, "panel", "fsdp"),
            P(None, "panel", "fsdp"),
        ),
        out_specs=(
            P(None, ("fsdp", "panel"), None),
            P(None, "panel", "fsdp"),
            P(None, "panel", "fsdp"),
            P(None, ("fsdp", "panel"), None),
        ),
        check_vma=False,
    )
```
